32 devices in a mesh: shot: 2 (over x), freq: 16 (over z, y, core).
Axes of the slice: x: 2, y: 2, z: 4, core: 2. Of those that a mesh axis runs over, the one named last changes fastest.
Arguments:
- receiver_data: float32 [64, 2, 32, 1024], P(('shot', 'freq')), parts along dimension 0, may hold values from -6 to 6
- source_spectrum: float32 [32, 2], P('freq'), may hold values from -4 to 4
- filter_taps: float32 [32, 4, 6], P('freq'), may hold values from -1.5 to 1.5, as said below
- slowness: float32 [16, 32, 1024], P('freq'), may hold values from 0.5 to 2
- depth_owner: int32 [6], P('shot'), parts along dimension 0, may hold values from 0 to 15
- source_position: int32 [4], P('shot'), parts along dimension 0, may hold values from 0 to 31
Outputs:
- migrated_image: float32 [32, 32, 1024], P(('shot', 'freq')), parts along dimension 0
The draws below stay inside these ranges and needn't reach their ends.
There are 2 independent parts, one for each index of `shot`. The reference program is written for one: setup_inputs(seed, part) draws one part's arguments, and reference() takes and returns one part's arrays. A program takes and returns all parts, laid end to end along the dimension named above; an argument that names none is the same for every part. Nothing has to cross between parts.
Inputs may be any that keep to these rules, and one draw needn't show every extreme that they name: `filter_taps`: each frequency and direction holds three complex taps.
All inputs are finite; a program needn't handle non-finite values.
Results may differ from the reference program's by a relative error of at most 0.0001.
Values sent between devices are 32-bit elements; how exact they have to be, the bound alone decides.
A program may use at most 64 MiB of HBM per device.

```python
import math
import jax
import jax.numpy as jnp
from jax import lax

NX = 32
NY = 1024
STEPS = 3
NF = 32
SLABS = 16


def draw_filter_taps(key, part):
    keys = jax.random.split(jax.random.fold_in(key, 17), 5)
    shape = (NF, 4)
    angles = jax.random.uniform(keys[0], shape, jnp.float32, -math.pi, math.pi)
    first_re = jax.random.uniform(keys[1], shape, jnp.float32, 0.04, 0.1)
    first_im = jax.random.uniform(keys[2], shape, jnp.float32, -0.1, 0.1)
    second_re = jax.random.uniform(keys[3], shape, jnp.float32, 0.02, 0.04)
    second_im = jax.random.uniform(keys[4], shape, jnp.float32, -0.04, 0.04)
    rot_re = jnp.cos(angles)
    rot_im = jnp.sin(angles)
    inner_re = rot_re * first_re - rot_im * first_im
    inner_im = rot_re * first_im + rot_im * first_re
    outer_re = rot_re * second_re - rot_im * second_im
    outer_im = rot_re * second_im + rot_im * second_re
    centre_re = rot_re - 2.0 * inner_re - 2.0 * outer_re
    centre_im = rot_im - 2.0 * inner_im - 2.0 * outer_im
    return jnp.stack([centre_re, centre_im, inner_re, inner_im, outer_re, outer_im], axis=-1).astype(jnp.float32)


def levels(rng, shape, shards, low, high):
    def one(dim, parts):
        steps = jax.random.uniform(jax.random.fold_in(jax.random.fold_in(rng, 6), dim), (parts,), jnp.float32, low / len(shards), high / len(shards))
        return jnp.repeat(jnp.exp(steps), shape[dim] // parts).reshape((-1,) + (1,) * (len(shape) - dim - 1))

    factor_of = one(*shards[0])
    for cut in shards[1:]:
        factor_of = factor_of * one(*cut)
    return factor_of


def gaussian(rng, dims, spread, most, cuts=(), kind=jnp.bfloat16):
    drawn = spread * jax.random.normal(rng, dims, jnp.float32)
    if cuts:
        drawn = drawn * levels(rng, dims, cuts, -0.22, 0.18)
    return jnp.clip(drawn, -most, most).astype(kind)


def setup_inputs(seed: int = 0, part: int = 0) -> dict:
    splits = jax.random.split(jax.random.key(seed), 7)
    own_keys = jax.random.split(jax.random.fold_in(splits[6], part), 7)
    receiver_data = gaussian(own_keys[0], (NF, 2, NX, NY), 1.0, 6.0, ((0, 16),), jnp.float32)
    source_spectrum = gaussian(splits[1], (NF, 2), 1.0, 4.0, ((0, 16),), jnp.float32)
    filter_taps = draw_filter_taps(jax.random.fold_in(splits[6], 71), part)
    slowness = jnp.clip(jnp.exp(math.log(2.0) - 1.3862944 * jax.random.uniform(splits[3], (SLABS, NX, NY), jnp.float32) ** levels(splits[3], (SLABS, NX, NY), ((0, 16),), -0.2, 0.2)), 0.5, 2.0)
    depth_owner = jax.random.randint(own_keys[4], (STEPS,), 0, SLABS).astype(jnp.int32)
    source_position = jax.random.randint(own_keys[5], (2,), 0, NX).astype(jnp.int32)
    return {"receiver_data": receiver_data, "source_spectrum": source_spectrum, "filter_taps": filter_taps, "slowness": slowness, "depth_owner": depth_owner, "source_position": source_position}


lens_rate = 3.0
wave_rate = 0.5
directions = ((1, 0), (0, 1), (1, 1), (1, -1))

def source_start(spectrum, position, freq_index, freq_total, height, breadth):
    src_row = position[0].astype(jnp.float32)
    src_col = position[1].astype(jnp.float32)
    row_axis = jnp.arange(height, dtype=jnp.float32)[:, None]
    col_axis = jnp.arange(breadth, dtype=jnp.float32)[None, :]
    distance = jnp.sqrt((row_axis - src_row) ** 2 + (col_axis - src_col) ** 2 + 1.0)
    amplitude = 1.0 / (1.0 + distance / (height / 4.0))
    wavenumber = (freq_index.astype(jnp.float32) + 1.0) * (wave_rate / freq_total)
    phase_map = wavenumber[:, None, None] * distance[None]
    base_re = amplitude[None] * jnp.cos(phase_map)
    base_im = -amplitude[None] * jnp.sin(phase_map)
    wave_re = spectrum[:, 0][:, None, None]
    wave_im = spectrum[:, 1][:, None, None]
    return jnp.stack([wave_re * base_re - wave_im * base_im, wave_re * base_im + wave_im * base_re], axis=1)

def complex_mul(values, coef_re, coef_im):
    coef_re = coef_re[:, None, None]
    coef_im = coef_im[:, None, None]
    return jnp.stack([values[:, 0] * coef_re - values[:, 1] * coef_im, values[:, 0] * coef_im + values[:, 1] * coef_re], axis=1)

def thin_lens(wavefield, layer_slab, freq_index, freq_total, handed):
    phases = (freq_index.astype(jnp.float32) + 1.0)[:, None, None] * (lens_rate / freq_total) * layer_slab[None]
    rot_re = jnp.cos(phases)
    rot_im = handed * jnp.sin(phases)
    part_re = wavefield[:, 0]
    part_im = wavefield[:, 1]
    return jnp.stack([part_re * rot_re - part_im * rot_im, part_re * rot_im + part_im * rot_re], axis=1)

def directional(wavefield, coeffs, step_x, step_y, handed):
    height = wavefield.shape[2]
    breadth = wavefield.shape[3]
    padded = jnp.pad(wavefield, ((0, 0), (0, 0), (2, 2), (2, 2)))

    def adjacent(offset):
        return padded[:, :, 2 + offset * step_x:2 + offset * step_x + height, 2 + offset * step_y:2 + offset * step_y + breadth]
    inner_pair = adjacent(1) + adjacent(-1)
    outer_pair = adjacent(2) + adjacent(-2)
    result = complex_mul(wavefield, coeffs[:, 0], handed * coeffs[:, 1])
    result = result + complex_mul(inner_pair, coeffs[:, 2], handed * coeffs[:, 3])
    return result + complex_mul(outer_pair, coeffs[:, 4], handed * coeffs[:, 5])

def depth_step(source, receiver, layer_slab, filter_taps, freq_index, freq_total):
    source = thin_lens(source, layer_slab, freq_index, freq_total, -1.0)
    receiver = thin_lens(receiver, layer_slab, freq_index, freq_total, 1.0)
    for direction, (step_x, step_y) in enumerate(directions):
        source = directional(source, filter_taps[:, direction], step_x, step_y, 1.0)
        receiver = directional(receiver, filter_taps[:, direction], step_x, step_y, -1.0)
    return (source, receiver)

def reference(receiver_data, source_spectrum, filter_taps, slowness, depth_owner, source_position):
    freq_index = jnp.arange(NF, dtype=jnp.int32)
    source = source_start(source_spectrum, source_position, freq_index, NF, NX, NY)
    receiver = receiver_data
    slab_ids = jnp.arange(SLABS, dtype=jnp.int32)
    migrated = jnp.zeros((SLABS, NX, NY), jnp.float32)
    for level in range(STEPS):
        layer_slab = lax.dynamic_index_in_dim(slowness, depth_owner[level].astype(jnp.int32), 0, keepdims=False)
        source, receiver = depth_step(source, receiver, layer_slab, filter_taps, freq_index, NF)
        correlation = lax.optimization_barrier(jnp.sum(source[:, 0] * receiver[:, 0] + source[:, 1] * receiver[:, 1], axis=0)) / math.sqrt(NF)
        owner_mask = (slab_ids == depth_owner[level]).astype(jnp.float32)
        migrated = migrated + owner_mask[:, None, None] * correlation[None]
    return migrated
```

```python
import functools
import math

import jax
import jax.numpy as jnp
from jax import lax
from jax.experimental import pallas as pl
from jax.experimental.pallas import tpu as pltpu
from jax.sharding import PartitionSpec as P

lens_rate = 3.0
wave_rate = 0.5
MESH = pl.DeviceIdType.MESH
SUB = 8
LANE = 128
TOP = 8


def sincos(x):
    k = jnp.floor(x * (2.0 / math.pi) + 0.5)
    r = x - k * 1.5703125
    r = r - k * 4.837512969970703125e-4
    r = r - k * 7.54978995489188216e-8
    q = k.astype(jnp.int32)
    z = r * r
    s = r + r * z * (-1.6666654611e-1 + z * (8.3321608736e-3 - z * 1.9515295891e-4))
    c = 1.0 - 0.5 * z + z * z * (
        4.166664568298827e-2 + z * (-1.388731625493765e-3 + z * 2.443315711809948e-5)
    )
    swap = (q & 1) == 1
    sin = jnp.where(swap, c, s)
    cos = jnp.where(swap, s, c)
    sin = jnp.where((q & 2) == 2, -sin, sin)
    cos = jnp.where(((q + 1) & 2) == 2, -cos, cos)
    return sin, cos


def kernel(
    n,
    owner,
    position,
    spectrum,
    taps,
    recv_hbm,
    slow,
    out,
    rbuf,
    fx,
    fy,
    all_slow,
    picked,
    slabs,
    parts,
    red,
    image,
    load_sem,
    a_send,
    a_recv,
    b_send,
    b_recv,
    c_send,
    c_recv,
    d_send,
    d_recv,
):
    me = lax.axis_index("freq")
    steps = owner.shape[0]
    fl = rbuf.shape[0]
    height = rbuf.shape[2]
    breadth = rbuf.shape[3]
    nb = breadth // LANE
    nrt = height // SUB
    cr = slow.shape[1]
    freq_total = n * fl
    first = me * fl

    def peer(i):
        return lax.rem(me + i, n)

    def remote(src, dst, send, recv, to):
        return pltpu.make_async_remote_copy(
            src_ref=src, dst_ref=dst, send_sem=send, recv_sem=recv,
            device_id={"freq": to}, device_id_type=MESH,
        )

    load = pltpu.make_async_copy(recv_hbm, rbuf, load_sem)
    load.start()
    barrier = pltpu.get_barrier_semaphore()
    for i in range(1, n):
        pl.semaphore_signal(barrier, inc=1, device_id={"freq": peer(i)}, device_id_type=MESH)
    pl.semaphore_wait(barrier, n - 1)

    a_copies = [
        remote(slow.at[peer(i)], all_slow.at[me], a_send.at[i], a_recv.at[i], peer(i))
        for i in range(1, n)
    ]
    for copy in a_copies:
        copy.start()
    all_slow[me] = slow[me]

    def pieces(rt, cb):
        row = (rt * nb + cb) * SUB
        size = min(cr, SUB)
        return [((row + o) // cr, (row + o) % cr, size, o) for o in range(0, SUB, size)]

    def tile_load(ref, rt, cb):
        got = [ref[c, r : r + m] for c, r, m, _ in pieces(rt, cb)]
        return got[0] if len(got) == 1 else jnp.concatenate(got, axis=0)

    def tile_store(ref, rt, cb, value):
        for c, r, m, o in pieces(rt, cb):
            ref[c, r : r + m] = value[o : o + m]

    def rows(rt, k=0):
        start = TOP + rt * SUB + k
        return slice(start, start + SUB)

    lanes = lax.broadcasted_iota(jnp.int32, (SUB, LANE), 1)
    subs = lax.broadcasted_iota(jnp.int32, (SUB, LANE), 0)
    zero = jnp.zeros((SUB, LANE), jnp.float32)

    @pl.loop(0, fl * 2)
    def _(field):
        for part in range(2):
            for cb in range(nb):
                for buf in (fx, fy):
                    buf[field, part, cb, 0:TOP] = zero
                    buf[field, part, cb, TOP + height : 2 * TOP + height] = zero

    src_row = position[0].astype(jnp.float32)
    src_col = position[1].astype(jnp.float32)
    for rt in range(nrt):
        for cb in range(nb):
            row = (subs + rt * SUB).astype(jnp.float32) - src_row
            col = (lanes + cb * LANE).astype(jnp.float32) - src_col
            distance = jnp.sqrt(row * row + col * col + 1.0)
            amplitude = 1.0 / (1.0 + distance / (height / 4.0))
            for f in range(fl):
                number = ((first + f).astype(jnp.float32) + 1.0) * (wave_rate / freq_total)
                sin, cos = sincos(number * distance)
                base_re = amplitude * cos
                base_im = -amplitude * sin
                wr = spectrum[f, 0]
                wi = spectrum[f, 1]
                fx[2 * f, 0, cb, rows(rt)] = wr * base_re - wi * base_im
                fx[2 * f, 1, cb, rows(rt)] = wr * base_im + wi * base_re
    load.wait()
    for f in range(fl):
        for rt in range(nrt):
            for cb in range(nb):
                at = (slice(rt * SUB, rt * SUB + SUB), slice(cb * LANE, cb * LANE + LANE))
                fx[2 * f + 1, 0, cb, rows(rt)] = rbuf[(f, 0) + at]
                fx[2 * f + 1, 1, cb, rows(rt)] = -rbuf[(f, 1) + at]

    for copy in a_copies:
        copy.wait_recv()
    b_copies = []
    for t in range(steps):
        picked[t] = all_slow[owner[t]]
        slabs[t, me] = picked[t]
        sends = [
            remote(picked.at[t], slabs.at[t, me], b_send.at[t, i], b_recv.at[t, i], peer(i))
            for i in range(1, n)
        ]
        for copy in sends:
            copy.start()
        b_copies.append(sends)

    def column_shift(get, s):
        memo = {}

        def rolled(cb):
            if cb < 0 or cb >= nb:
                return zero
            if cb not in memo:
                memo[cb] = pltpu.roll(get(cb), (-s) % LANE, 1)
            return memo[cb]

        def at(cb):
            if s > 0:
                return jnp.where(lanes >= LANE - s, rolled(cb + 1), rolled(cb))
            return jnp.where(lanes < -s, rolled(cb - 1), rolled(cb))

        return at

    def combine(c, x, one, two):
        (xr, xi), (pr, pi), (qr, qi) = x, one, two
        re = (c[0] * xr - c[1] * xi) + (c[2] * pr - c[3] * pi) + (c[4] * qr - c[5] * qi)
        im = (c[0] * xi + c[1] * xr) + (c[2] * pi + c[3] * pr) + (c[4] * qi + c[5] * qr)
        return re, im

    def coefficients(f, d):
        return [taps[f, d, j] for j in range(6)]

    def lens(buf, slab):
        @pl.loop(0, fl)
        def _(f):
            rate = ((first + f).astype(jnp.float32) + 1.0) * (lens_rate / freq_total)
            for rt in range(nrt):
                for cb in range(nb):
                    sin, cos = sincos(rate * tile_load(slab, rt, cb))
                    for s in range(2):
                        re = buf[2 * f + s, 0, cb, rows(rt)]
                        im = buf[2 * f + s, 1, cb, rows(rt)]
                        buf[2 * f + s, 0, cb, rows(rt)] = re * cos + im * sin
                        buf[2 * f + s, 1, cb, rows(rt)] = im * cos - re * sin

    def rows_then_columns(src, dst):
        @pl.loop(0, fl * 2)
        def _(field):
            f = lax.div(field, 2)
            c0 = coefficients(f, 0)
            c1 = coefficients(f, 1)
            for rt in range(nrt):
                memo = {}

                def down(cb):
                    if cb not in memo:
                        x = [src[field, p, cb, rows(rt)] for p in range(2)]
                        one = [src[field, p, cb, rows(rt, 1)] + src[field, p, cb, rows(rt, -1)] for p in range(2)]
                        two = [src[field, p, cb, rows(rt, 2)] + src[field, p, cb, rows(rt, -2)] for p in range(2)]
                        memo[cb] = combine(c0, x, one, two)
                    return memo[cb]

                moved = [
                    {s: column_shift(lambda cb, p=p: down(cb)[p], s) for s in (1, -1, 2, -2)}
                    for p in range(2)
                ]
                for cb in range(nb):
                    one = [moved[p][1](cb) + moved[p][-1](cb) for p in range(2)]
                    two = [moved[p][2](cb) + moved[p][-2](cb) for p in range(2)]
                    re, im = combine(c1, down(cb), one, two)
                    dst[field, 0, cb, rows(rt)] = re
                    dst[field, 1, cb, rows(rt)] = im

    def slanted(src, field, c, rt, side):
        moved = [
            {
                s: column_shift(lambda cb, p=p, s=s: src[field, p, cb, rows(rt, s)], s * side)
                for s in (1, -1, 2, -2)
            }
            for p in range(2)
        ]

        def at(cb):
            x = [src[field, p, cb, rows(rt)] for p in range(2)]
            one = [moved[p][1](cb) + moved[p][-1](cb) for p in range(2)]
            two = [moved[p][2](cb) + moved[p][-2](cb) for p in range(2)]
            return combine(c, x, one, two)

        return at

    def first_slant(src, dst):
        @pl.loop(0, fl * 2)
        def _(field):
            c = coefficients(lax.div(field, 2), 2)
            for rt in range(nrt):
                at = slanted(src, field, c, rt, 1)
                for cb in range(nb):
                    re, im = at(cb)
                    dst[field, 0, cb, rows(rt)] = re
                    dst[field, 1, cb, rows(rt)] = im

    def second_slant(src, dst, part, keep):
        for f in range(fl):
            c = coefficients(f, 3)
            for rt in range(nrt):
                source = slanted(src, 2 * f, c, rt, -1)
                receiver = slanted(src, 2 * f + 1, c, rt, -1)
                for cb in range(nb):
                    sr, si = source(cb)
                    rr, ri = receiver(cb)
                    if keep:
                        dst[2 * f, 0, cb, rows(rt)] = sr
                        dst[2 * f, 1, cb, rows(rt)] = si
                        dst[2 * f + 1, 0, cb, rows(rt)] = rr
                        dst[2 * f + 1, 1, cb, rows(rt)] = ri
                    term = sr * rr - si * ri
                    if f > 0:
                        term = tile_load(part, rt, cb) + term
                    tile_store(part, rt, cb, term)

    now, later = fx, fy
    c_copies = []
    for t in range(steps):
        for copy in b_copies[t]:
            copy.wait_recv()
        lens(now, slabs.at[t])
        rows_then_columns(now, later)
        first_slant(later, now)
        second_slant(now, later, parts.at[t], t < steps - 1)
        now, later = later, now
        sends = [
            remote(parts.at[t, peer(i)], red.at[t, me], c_send.at[t, i], c_recv.at[t, i], peer(i))
            for i in range(1, n)
        ]
        for copy in sends:
            copy.start()
        red[t, me] = parts[t, me]
        c_copies.append(sends)

    sums = []
    for t in range(steps):
        for copy in c_copies[t]:
            copy.wait_recv()
        total = red[t, 0]
        for i in range(1, n):
            total = total + red[t, i]
        sums.append(total / math.sqrt(freq_total))
    for k in range(n):
        value = sums[0] * (owner[0] == k).astype(jnp.float32)
        for t in range(1, steps):
            value = value + sums[t] * (owner[t] == k).astype(jnp.float32)
        image[k] = value
    d_copies = [
        remote(image.at[peer(i)], out.at[me], d_send.at[i], d_recv.at[i], peer(i))
        for i in range(1, n)
    ]
    for copy in d_copies:
        copy.start()
    out[me] = image[me]
    for copy in d_copies:
        copy.wait_recv()
    for copy in a_copies + sum(b_copies, []) + sum(c_copies, []) + d_copies:
        copy.wait_send()


def local(n, receiver_data, source_spectrum, filter_taps, slowness, depth_owner, source_position):
    fl, _, height, breadth = receiver_data.shape
    steps = depth_owner.shape[0]
    nb = breadth // LANE
    nrt = height // SUB
    cr = height * nb // n
    slab = slowness[0].reshape(nrt, SUB, nb, LANE).transpose(0, 2, 1, 3).reshape(n, cr, LANE)
    chunks = (n, cr, LANE)
    smem = pl.BlockSpec(memory_space=pltpu.SMEM)
    vmem = pl.BlockSpec(memory_space=pltpu.VMEM)
    fields = (2 * fl, 2, nb, height + 2 * TOP, LANE)
    dma = pltpu.SemaphoreType.DMA
    result = pl.pallas_call(
        functools.partial(kernel, n),
        out_shape=jax.ShapeDtypeStruct(chunks, jnp.float32),
        in_specs=[smem, smem, smem, smem, pl.BlockSpec(memory_space=pl.ANY), vmem],
        out_specs=vmem,
        scratch_shapes=[
            pltpu.VMEM(receiver_data.shape, jnp.float32),
            pltpu.VMEM(fields, jnp.float32),
            pltpu.VMEM(fields, jnp.float32),
            pltpu.VMEM(chunks, jnp.float32),
            pltpu.VMEM((steps, cr, LANE), jnp.float32),
            pltpu.VMEM((steps,) + chunks, jnp.float32),
            pltpu.VMEM((steps,) + chunks, jnp.float32),
            pltpu.VMEM((steps,) + chunks, jnp.float32),
            pltpu.VMEM(chunks, jnp.float32),
            dma,
            dma((n,)),
            dma((n,)),
            dma((steps, n)),
            dma((steps, n)),
            dma((steps, n)),
            dma((steps, n)),
            dma((n,)),
            dma((n,)),
        ],
        compiler_params=pltpu.CompilerParams(
            collective_id=0, has_side_effects=True, vmem_limit_bytes=48 * 1024 * 1024
        ),
        name="migrate",
    )(depth_owner, source_position, source_spectrum, filter_taps, receiver_data, slab)
    image = result.reshape(nrt, nb, SUB, LANE).transpose(0, 2, 1, 3)
    return image.reshape(1, height, breadth)


def solution(mesh):
    return jax.shard_map(
        functools.partial(local, mesh.shape["freq"]),
        mesh=mesh,
        in_specs=(
            P(("shot", "freq"), None, None, None),
            P("freq", None),
            P("freq", None, None),
            P("freq", None, None),
            P("shot"),
            P("shot"),
        ),
        out_specs=P(("shot", "freq"), None, None),
        check_vma=False,
    )
```

```python
import functools
import math

import jax
import jax.numpy as jnp
from jax import lax
from jax.experimental import pallas as pl
from jax.experimental.pallas import tpu as pltpu
from jax.sharding import PartitionSpec as P

lens_rate = 3.0
wave_rate = 0.5
MESH = pl.DeviceIdType.MESH
SUB = 8
LANE = 128
TOP = 8


def sincos(x):
    k = jnp.floor(x * (2.0 / math.pi) + 0.5)
    r = x - k * 1.5703125
    r = r - k * 4.837512969970703125e-4
    r = r - k * 7.54978995489188216e-8
    q = k.astype(jnp.int32)
    z = r * r
    s = r + r * z * (-1.6666654611e-1 + z * (8.3321608736e-3 - z * 1.9515295891e-4))
    c = 1.0 - 0.5 * z + z * z * (
        4.166664568298827e-2 + z * (-1.388731625493765e-3 + z * 2.443315711809948e-5)
    )
    swap = (q & 1) == 1
    sin = jnp.where(swap, c, s)
    cos = jnp.where(swap, s, c)
    sin = jnp.where((q & 2) == 2, -sin, sin)
    cos = jnp.where(((q + 1) & 2) == 2, -cos, cos)
    return sin, cos


def kernel(
    n,
    owner,
    position,
    spectrum,
    taps,
    recv_hbm,
    slow,
    out,
    rbuf,
    fx,
    fy,
    all_slow,
    picked,
    slabs,
    parts,
    red,
    image,
    load_sem,
    own_sem,
    a_send,
    a_recv,
    b_send,
    b_recv,
    c_send,
    c_recv,
    d_send,
    d_recv,
):
    me = lax.axis_index("freq")
    steps = owner.shape[0]
    fl = rbuf.shape[0]
    height = rbuf.shape[2]
    breadth = rbuf.shape[3]
    nb = breadth // LANE
    nrt = height // SUB
    cr = slow.shape[1]
    freq_total = n * fl
    first = me * fl

    def peer(i):
        if n & (n - 1):
            return lax.rem(me + i, n)
        to = 0
        for b in range(n.bit_length() - 1):
            bit = lax.rem(lax.div(me, 1 << b), 2)
            to = to + (1 << b) * (1 - bit if i >> b & 1 else bit)
        return to

    partners = [peer(i) for i in range(n)]
    rounds = range(n - 1, 0, -1)

    def remote(src, dst, send, recv, to):
        return pltpu.make_async_remote_copy(
            src_ref=src, dst_ref=dst, send_sem=send, recv_sem=recv,
            device_id={"freq": to}, device_id_type=MESH,
        )

    load = pltpu.make_async_copy(recv_hbm, rbuf, load_sem)
    load.start()
    barrier = pltpu.get_barrier_semaphore()
    for i in rounds:
        pl.semaphore_signal(barrier, inc=1, device_id={"freq": partners[i]}, device_id_type=MESH)
    pl.semaphore_wait(barrier, n - 1)

    a_copies = [
        remote(slow.at[partners[i]], all_slow.at[me], a_send.at[i], a_recv.at[i], partners[i])
        for i in rounds
    ]
    for copy in a_copies:
        copy.start()
    own = pltpu.make_async_copy(slow.at[me], all_slow.at[me], own_sem)
    own.start()

    def pieces(rt, cb):
        row = (rt * nb + cb) * SUB
        size = min(cr, SUB)
        return [((row + o) // cr, (row + o) % cr, size, o) for o in range(0, SUB, size)]

    def tile_load(ref, rt, cb):
        got = [ref[c, r : r + m] for c, r, m, _ in pieces(rt, cb)]
        return got[0] if len(got) == 1 else jnp.concatenate(got, axis=0)

    def tile_store(ref, rt, cb, value):
        for c, r, m, o in pieces(rt, cb):
            ref[c, r : r + m] = value[o : o + m]

    def rows(rt, k=0):
        start = TOP + rt * SUB + k
        return slice(start, start + SUB)

    lanes = lax.broadcasted_iota(jnp.int32, (SUB, LANE), 1)
    subs = lax.broadcasted_iota(jnp.int32, (SUB, LANE), 0)
    zero = jnp.zeros((SUB, LANE), jnp.float32)

    @pl.loop(0, fl * 2)
    def _(field):
        for part in range(2):
            for cb in range(nb):
                for buf in (fx, fy):
                    buf[field, part, cb, 0:TOP] = zero
                    buf[field, part, cb, TOP + height : 2 * TOP + height] = zero

    src_row = position[0].astype(jnp.float32)
    src_col = position[1].astype(jnp.float32)
    for rt in range(nrt):
        for cb in range(nb):
            row = (subs + rt * SUB).astype(jnp.float32) - src_row
            col = (lanes + cb * LANE).astype(jnp.float32) - src_col
            distance = jnp.sqrt(row * row + col * col + 1.0)
            amplitude = 1.0 / (1.0 + distance / (height / 4.0))
            for f in range(fl):
                number = ((first + f).astype(jnp.float32) + 1.0) * (wave_rate / freq_total)
                sin, cos = sincos(number * distance)
                base_re = amplitude * cos
                base_im = -amplitude * sin
                wr = spectrum[f, 0]
                wi = spectrum[f, 1]
                fx[2 * f, 0, cb, rows(rt)] = wr * base_re - wi * base_im
                fx[2 * f, 1, cb, rows(rt)] = wr * base_im + wi * base_re
    load.wait()
    for f in range(fl):
        for rt in range(nrt):
            for cb in range(nb):
                at = (slice(rt * SUB, rt * SUB + SUB), slice(cb * LANE, cb * LANE + LANE))
                fx[2 * f + 1, 0, cb, rows(rt)] = rbuf[(f, 0) + at]
                fx[2 * f + 1, 1, cb, rows(rt)] = -rbuf[(f, 1) + at]

    own.wait()
    for copy in a_copies:
        copy.wait_recv()
    b_copies = []
    for t in range(steps):
        value = all_slow[owner[t]]
        picked[t] = value
        slabs[t, me] = value
        sends = [
            remote(picked.at[t], slabs.at[t, me], b_send.at[t, i], b_recv.at[t, i], partners[i])
            for i in rounds
        ]
        b_copies.append(sends)

    def begin(copies):
        for copy in copies:
            copy.start()

    def left(copies):
        for copy in copies:
            copy.wait_send()

    begin(b_copies[0])
    left(b_copies[0])
    if steps > 1:
        begin(b_copies[1])

    def column_shift(get, s):
        memo = {}

        def rolled(cb):
            if cb < 0 or cb >= nb:
                return zero
            if cb not in memo:
                memo[cb] = pltpu.roll(get(cb), (-s) % LANE, 1)
            return memo[cb]

        def at(cb):
            if s > 0:
                return jnp.where(lanes >= LANE - s, rolled(cb + 1), rolled(cb))
            return jnp.where(lanes < -s, rolled(cb - 1), rolled(cb))

        return at

    def combine(c, x, one, two):
        (xr, xi), (pr, pi), (qr, qi) = x, one, two
        re = (c[0] * xr - c[1] * xi) + (c[2] * pr - c[3] * pi) + (c[4] * qr - c[5] * qi)
        im = (c[0] * xi + c[1] * xr) + (c[2] * pi + c[3] * pr) + (c[4] * qi + c[5] * qr)
        return re, im

    def coefficients(f, d):
        return [taps[f, d, j] for j in range(6)]

    def lens(buf, slab):
        @pl.loop(0, fl)
        def _(f):
            rate = ((first + f).astype(jnp.float32) + 1.0) * (lens_rate / freq_total)
            for rt in range(nrt):
                for cb in range(nb):
                    sin, cos = sincos(rate * tile_load(slab, rt, cb))
                    for s in range(2):
                        re = buf[2 * f + s, 0, cb, rows(rt)]
                        im = buf[2 * f + s, 1, cb, rows(rt)]
                        buf[2 * f + s, 0, cb, rows(rt)] = re * cos + im * sin
                        buf[2 * f + s, 1, cb, rows(rt)] = im * cos - re * sin

    def rows_then_columns(src, dst):
        @pl.loop(0, fl * 2)
        def _(field):
            f = lax.div(field, 2)
            c0 = coefficients(f, 0)
            c1 = coefficients(f, 1)
            for rt in range(nrt):
                memo = {}

                def down(cb):
                    if cb not in memo:
                        x = [src[field, p, cb, rows(rt)] for p in range(2)]
                        one = [src[field, p, cb, rows(rt, 1)] + src[field, p, cb, rows(rt, -1)] for p in range(2)]
                        two = [src[field, p, cb, rows(rt, 2)] + src[field, p, cb, rows(rt, -2)] for p in range(2)]
                        memo[cb] = combine(c0, x, one, two)
                    return memo[cb]

                moved = [
                    {s: column_shift(lambda cb, p=p: down(cb)[p], s) for s in (1, -1, 2, -2)}
                    for p in range(2)
                ]
                for cb in range(nb):
                    one = [moved[p][1](cb) + moved[p][-1](cb) for p in range(2)]
                    two = [moved[p][2](cb) + moved[p][-2](cb) for p in range(2)]
                    re, im = combine(c1, down(cb), one, two)
                    dst[field, 0, cb, rows(rt)] = re
                    dst[field, 1, cb, rows(rt)] = im

    def slanted(src, field, c, rt, side):
        moved = [
            {
                s: column_shift(lambda cb, p=p, s=s: src[field, p, cb, rows(rt, s)], s * side)
                for s in (1, -1, 2, -2)
            }
            for p in range(2)
        ]

        def at(cb):
            x = [src[field, p, cb, rows(rt)] for p in range(2)]
            one = [moved[p][1](cb) + moved[p][-1](cb) for p in range(2)]
            two = [moved[p][2](cb) + moved[p][-2](cb) for p in range(2)]
            return combine(c, x, one, two)

        return at

    def first_slant(src, dst):
        @pl.loop(0, fl * 2)
        def _(field):
            c = coefficients(lax.div(field, 2), 2)
            for rt in range(nrt):
                at = slanted(src, field, c, rt, 1)
                for cb in range(nb):
                    re, im = at(cb)
                    dst[field, 0, cb, rows(rt)] = re
                    dst[field, 1, cb, rows(rt)] = im

    def second_slant(src, dst, part, keep):
        for rt in range(nrt):
            for f in range(fl):
                c = coefficients(f, 3)
                source = slanted(src, 2 * f, c, rt, -1)
                receiver = slanted(src, 2 * f + 1, c, rt, -1)
                for cb in range(nb):
                    sr, si = source(cb)
                    rr, ri = receiver(cb)
                    if keep:
                        dst[2 * f, 0, cb, rows(rt)] = sr
                        dst[2 * f, 1, cb, rows(rt)] = si
                        dst[2 * f + 1, 0, cb, rows(rt)] = rr
                        dst[2 * f + 1, 1, cb, rows(rt)] = ri
                    term = sr * rr - si * ri
                    if f > 0:
                        term = tile_load(part, rt, cb) + term
                    tile_store(part, rt, cb, term)

    now, later = fx, fy
    c_copies = []
    for t in range(steps):
        for copy in b_copies[t]:
            copy.wait_recv()
        if 0 < t < steps - 1:
            left(b_copies[t])
            begin(b_copies[t + 1])
        lens(now, slabs.at[t])
        rows_then_columns(now, later)
        first_slant(later, now)
        second_slant(now, later, parts.at[t], t < steps - 1)
        now, later = later, now
        sends = [
            remote(parts.at[t, partners[i]], red.at[t, me], c_send.at[t, i], c_recv.at[t, i], partners[i])
            for i in rounds
        ]
        for copy in sends:
            copy.start()
        red[t, me] = parts[t, me]
        c_copies.append(sends)

    sums = []
    for t in range(steps):
        for copy in c_copies[t]:
            copy.wait_recv()
        total = red[t, 0]
        for i in range(1, n):
            total = total + red[t, i]
        sums.append(total / math.sqrt(freq_total))
    for k in range(n):
        value = sums[0] * (owner[0] == k).astype(jnp.float32)
        for t in range(1, steps):
            value = value + sums[t] * (owner[t] == k).astype(jnp.float32)
        image[k] = value
    d_copies = [
        remote(image.at[partners[i]], out.at[me], d_send.at[i], d_recv.at[i], partners[i])
        for i in rounds
    ]
    for copy in d_copies:
        copy.start()
    out[me] = image[me]
    for copy in d_copies:
        copy.wait_recv()
    for copy in a_copies + b_copies[-1] * (steps > 1) + sum(c_copies, []) + d_copies:
        copy.wait_send()


def local(n, receiver_data, source_spectrum, filter_taps, slowness, depth_owner, source_position):
    fl, _, height, breadth = receiver_data.shape
    steps = depth_owner.shape[0]
    nb = breadth // LANE
    nrt = height // SUB
    cr = height * nb // n
    slab = slowness[0].reshape(nrt, SUB, nb, LANE).transpose(0, 2, 1, 3).reshape(n, cr, LANE)
    chunks = (n, cr, LANE)
    smem = pl.BlockSpec(memory_space=pltpu.SMEM)
    vmem = pl.BlockSpec(memory_space=pltpu.VMEM)
    hbm = pl.BlockSpec(memory_space=pltpu.HBM)
    fields = (2 * fl, 2, nb, height + 2 * TOP, LANE)
    dma = pltpu.SemaphoreType.DMA
    result = pl.pallas_call(
        functools.partial(kernel, n),
        out_shape=jax.ShapeDtypeStruct(chunks, jnp.float32),
        in_specs=[smem, smem, smem, smem, hbm, hbm],
        out_specs=vmem,
        scratch_shapes=[
            pltpu.VMEM(receiver_data.shape, jnp.float32),
            pltpu.VMEM(fields, jnp.float32),
            pltpu.VMEM(fields, jnp.float32),
            pltpu.VMEM(chunks, jnp.float32),
            pltpu.VMEM((steps, cr, LANE), jnp.float32),
            pltpu.VMEM((steps,) + chunks, jnp.float32),
            pltpu.VMEM((steps,) + chunks, jnp.float32),
            pltpu.VMEM((steps,) + chunks, jnp.float32),
            pltpu.VMEM(chunks, jnp.float32),
            dma,
            dma,
            dma((n,)),
            dma((n,)),
            dma((steps, n)),
            dma((steps, n)),
            dma((steps, n)),
            dma((steps, n)),
            dma((n,)),
            dma((n,)),
        ],
        compiler_params=pltpu.CompilerParams(
            collective_id=0, has_side_effects=True, vmem_limit_bytes=60 * 1024 * 1024
        ),
        name="migrate",
    )(depth_owner, source_position, source_spectrum, filter_taps, receiver_data, slab)
    image = result.reshape(nrt, nb, SUB, LANE).transpose(0, 2, 1, 3)
    return image.reshape(1, height, breadth)


def solution(mesh):
    return jax.shard_map(
        functools.partial(local, mesh.shape["freq"]),
        mesh=mesh,
        in_specs=(
            P(("shot", "freq"), None, None, None),
            P("freq", None),
            P("freq", None, None),
            P("freq", None, None),
            P("shot"),
            P("shot"),
        ),
        out_specs=P(("shot", "freq"), None, None),
        check_vma=False,
    )
```
